256 devices in a mesh: depth: 2 (over core), tile: 128 (over z, y, x).
Axes of the slice: x: 4, y: 4, z: 8, core: 2. Of those that a mesh axis runs over, the one named last changes fastest.
Arguments:
- object_layer_slices: float32 [2, 16384, 2, 2048], P('depth', 'tile'), may hold values from 0.2 to 1
- probe_wave: bfloat16 [256, 2, 256], replicated, may hold values from -5 to 5
- propagator: bfloat16 [256, 2, 256], replicated, may hold values from -0.25 to 0.25
- positions: int32 [128, 2, 5, 2], P('tile'), may hold values from 0 to 1792, as said below
- counts: int32 [128, 2], P('tile'), may hold values from 2 to 5
- measured: float32 [128, 2, 5, 256, 256], P('tile'), may hold values from 0 to 2
Outputs:
- object_gradient: float32 [2, 16384, 2, 2048], P('depth', 'tile')
The draws below stay inside these ranges and needn't reach their ends.
Inputs may be any that keep to these rules, and one draw needn't show every extreme that they name: Every window lies inside the object: on tile 0 the first component is 128 or more, on the last tile it is 0 or less; elsewhere it is at most 128, and the second component at most 1792. Slots at or beyond counts[t, b] also hold valid positions. Slots j < counts[t, b] of tile t and micro-batch b are live.
All inputs are finite; a program needn't handle non-finite values.
Results may differ from the reference program's by a relative error of at most 0.013.
Values may be sent and summed in bfloat16 or wider, within the bound.
No kernel may reach another device: no remote copies, remote signals or barrier semaphores. Data moves between devices by JAX's collectives and lax.ppermute only.
A program may use at most 192 MiB of HBM per device.

```python
import math
import jax
import jax.numpy as jnp
from jax import lax

P_SIZE = 256
M = 128
TW = 128
LW = 2048
MB = 2
CAP = 5
NS = 2
TILES = 128
NX = 16384
N_TILE = 128


def draw_positions(key, part):
    row_key, column_key = jax.random.split(jax.random.fold_in(key, 11))
    tile_numbers = jnp.arange(TILES, dtype=jnp.int32)[:, None, None]
    lowest = jnp.where(tile_numbers == 0, M, 0).astype(jnp.int32)
    highest = jnp.where(tile_numbers == TILES - 1, TW + M - P_SIZE, TW + 2 * M - P_SIZE).astype(jnp.int32)
    grid_shape = (TILES, MB, CAP)
    lowest = jnp.broadcast_to(lowest, grid_shape)
    highest = jnp.broadcast_to(highest, grid_shape)
    row_begin_points = jax.random.randint(row_key, grid_shape, lowest, highest + 1, dtype=jnp.int32)
    columns = jax.random.randint(column_key, grid_shape, 0, LW - P_SIZE + 1, dtype=jnp.int32)
    return jnp.stack([row_begin_points, columns], axis=-1)


def place_ends(array, key, low, high):
    longest = array.shape.index(max(array.shape))
    spots = []
    for shift in (0, 1):
        where = [jax.random.randint(jax.random.fold_in(key, axis), (), 0, length) for axis, length in enumerate(array.shape)]
        where[longest] = (where[longest] + shift) % array.shape[longest]
        spots.append(tuple(where))
    return array.at[spots[0]].set(low).at[spots[1]].set(high)


def block_scale(rng, shape, pieces, least, top_value):
    level, own = 1.0, jax.random.fold_in(rng, 6)
    for axis_at, shards_of in pieces:
        steps = jnp.exp(jax.random.uniform(jax.random.fold_in(own, axis_at), (shards_of,), jnp.float32, least / len(pieces), top_value / len(pieces)))
        level = level * jnp.repeat(steps, shape[axis_at] // shards_of).reshape([-1 if axis == axis_at else 1 for axis in range(len(shape))])
    return level


def noise(own_key, extent, deviation, limit, kind=jnp.bfloat16):
    values = jax.random.normal(own_key, extent, jnp.float32) * deviation
    return jnp.minimum(jnp.maximum(values, -limit), limit).astype(kind)


def setup_inputs(seed: int = 0) -> dict:
    key_list = jax.random.split(jax.random.key(seed), 7)
    object_layer_slices = jnp.clip(0.2 + 0.8 * jax.random.uniform(key_list[0], (NS, NX, 2, LW), jnp.float32) ** block_scale(key_list[0], (NS, NX, 2, LW), ((0, 2), (1, 128)), -0.2, 0.2), 0.2, 1.0)
    probe_wave = noise(key_list[1], (P_SIZE, 2, P_SIZE), 0.7, 5.0)
    propagator = noise(key_list[2], (P_SIZE, 2, P_SIZE), (2 * P_SIZE) ** -0.5, 0.25)
    positions = draw_positions(jax.random.fold_in(key_list[6], 71), 0)
    counts = place_ends(jax.random.randint(key_list[4], (TILES, MB), 2, CAP + 1), jax.random.fold_in(key_list[4], 1), 2, CAP).astype(jnp.int32)
    measured = jnp.clip(2.0 * jax.random.uniform(key_list[5], (TILES, MB, CAP, P_SIZE, P_SIZE), jnp.float32) ** block_scale(key_list[5], (TILES, MB, CAP, P_SIZE, P_SIZE), ((0, 128),), -0.2, 0.2), 0.0, 2.0)
    return dict(object_layer_slices=object_layer_slices, probe_wave=probe_wave, propagator=propagator, positions=positions, counts=counts, measured=measured)


def dft_table(side_cells):
    index_of_row = jnp.arange(side_cells, dtype=jnp.int32)
    phases = index_of_row[:, None] * index_of_row[None, :] % side_cells
    angles = phases.astype(jnp.float32) * (2.0 * math.pi / side_cells)
    factor = 1.0 / math.sqrt(side_cells)
    return jnp.stack([jnp.cos(angles) * factor, -jnp.sin(angles) * factor], axis=1).astype(jnp.bfloat16)

def conj_transpose(matrix):
    flipped = jnp.transpose(matrix, (2, 1, 0))
    return jnp.stack([flipped[:, 0], -flipped[:, 1]], axis=1)

def block_pair(matrix):
    real_part = matrix[:, 0]
    imag_part = matrix[:, 1]
    side_cells = real_part.shape[0]
    upper_half = jnp.stack([real_part, -imag_part], axis=2)
    lower_half = jnp.stack([imag_part, real_part], axis=2)
    leftward_block = jnp.stack([upper_half, lower_half], axis=1)
    right_block = jnp.transpose(leftward_block, (3, 2, 1, 0)).reshape(2 * side_cells, 2 * side_cells)
    return (leftward_block.reshape(2 * side_cells, 2 * side_cells), right_block)

def transform(blocks, wave_in):
    leftward_block, right_block = blocks
    slot_count, side_cells = (wave_in.shape[0], wave_in.shape[1])
    stacked_arrays = wave_in.reshape(slot_count, 2 * side_cells, side_cells).astype(jnp.float32)
    central_part = jnp.einsum('rj,tjg->trg', leftward_block.astype(jnp.float32), stacked_arrays, precision=lax.Precision.HIGHEST)
    central_part = central_part.astype(jnp.bfloat16).reshape(slot_count, side_cells, 2 * side_cells).astype(jnp.float32)
    result = jnp.einsum('cib,bk->cik', central_part, right_block.astype(jnp.float32), precision=lax.Precision.HIGHEST)
    return result.reshape(slot_count, side_cells, 2, side_cells)

def complex_product(first_wave, second_wave, conjugate):
    first_real = first_wave[..., 0, :].astype(jnp.float32)
    first_imag = first_wave[..., 1, :].astype(jnp.float32)
    second_real = second_wave[..., 0, :].astype(jnp.float32)
    second_imag = second_wave[..., 1, :].astype(jnp.float32)
    if conjugate:
        first_imag = -first_imag
    return jnp.stack([first_real * second_real - first_imag * second_imag, first_real * second_imag + first_imag * second_real], axis=-2)

def cut_windows(extended, placements):

    def single(placement):
        anchor = jnp.zeros((), jnp.int32)
        return lax.dynamic_slice(extended, (anchor, placement[0].astype(jnp.int32), anchor, placement[1].astype(jnp.int32)), (extended.shape[0], P_SIZE, 2, P_SIZE))
    return jax.vmap(single)(placements)

def add_patches(totals, patches, placements):
    for slot_no in range(patches.shape[0]):
        anchor = jnp.zeros((), jnp.int32)
        corner = (anchor, placements[slot_no, 0].astype(jnp.int32), anchor, placements[slot_no, 1].astype(jnp.int32))
        current = lax.dynamic_slice(totals, corner, patches.shape[1:])
        totals = lax.dynamic_update_slice(totals, current + patches[slot_no], corner)
    return totals

def forward_section(windows, wave_in, forward_list):
    entering = []
    leaving = None
    for slice_no in range(len(forward_list)):
        entering.append(wave_in)
        product = complex_product(windows[:, slice_no], wave_in, False).astype(jnp.bfloat16)
        leaving = transform(forward_list[slice_no], product)
        wave_in = leaving.astype(jnp.bfloat16)
    return (jnp.stack(entering, axis=0), leaving)

def backward_section(windows, entering, incoming, backward_list):
    patches = []
    for slice_no in reversed(range(len(backward_list))):
        spread = transform(backward_list[slice_no], incoming.astype(jnp.bfloat16)).astype(jnp.bfloat16)
        patches.insert(0, complex_product(entering[slice_no], spread, True))
        incoming = complex_product(windows[:, slice_no], spread, True)
    return jnp.stack(patches, axis=1)

def far_gradient(far_field, observed, live_slots):
    real_part = far_field[:, :, 0, :]
    imag_part = far_field[:, :, 1, :]
    weight = live_slots.astype(jnp.float32)[:, None, None]
    misfit = weight * (real_part * real_part + imag_part * imag_part - observed)
    return jnp.stack([misfit * real_part, misfit * imag_part], axis=2)

def reference(object_layer_slices, probe_wave, propagator, positions, counts, measured):
    all_slices = object_layer_slices.shape[0]
    detector = dft_table(P_SIZE)
    forward_list = [block_pair(propagator)] * (all_slices - 1) + [block_pair(detector)]
    backward_list = [block_pair(conj_transpose(propagator))] * (all_slices - 1) + [block_pair(conj_transpose(detector))]
    padded = jnp.pad(object_layer_slices, ((0, 0), (M, M), (0, 0), (0, 0)))
    start_wave = jnp.broadcast_to(probe_wave, (CAP, P_SIZE, 2, P_SIZE))

    def per_tile(totals, inputs):
        tile_no, tile_places, tile_counts, tile_measured = inputs
        first_row = (tile_no * TW).astype(jnp.int32)
        extended = lax.dynamic_slice_in_dim(padded, first_row, TW + 2 * M, 1)
        tile_sums = jnp.zeros(extended.shape, jnp.float32)
        for batch_no in range(MB):
            placements = tile_places[batch_no]
            live_slots = jnp.arange(CAP, dtype=jnp.int32) < tile_counts[batch_no]
            windows = cut_windows(extended, placements)
            entering, far_field = forward_section(windows, start_wave, forward_list)
            incoming = far_gradient(far_field, tile_measured[batch_no], live_slots)
            patches = backward_section(windows, entering, incoming, backward_list)
            tile_sums = add_patches(tile_sums, patches, placements)
        current = lax.dynamic_slice_in_dim(totals, first_row, TW + 2 * M, 1)
        totals = lax.dynamic_update_slice_in_dim(totals, current + tile_sums, first_row, 1)
        return (totals, None)
    totals = jnp.zeros(padded.shape, jnp.float32)
    tile_numbers = jnp.arange(N_TILE, dtype=jnp.int32)
    totals, ignored = lax.scan(per_tile, totals, (tile_numbers, positions, counts, measured))
    return totals[:, M:M + N_TILE * TW]
```

```python
import jax
import jax.numpy as jnp
import numpy as np
from jax import lax
from jax.experimental import pallas as pl
from jax.experimental.pallas import tpu as pltpu
from jax.sharding import PartitionSpec as P

SIDE = 256
M = 128
CAP = 5
LW = 2048
LANES = 128
WIDE = SIDE + LANES
BLOCKS = LW // LANES
GROUP = 8
MIB = 1024 * 1024


def dft_planes():
    n = np.arange(SIDE)
    angles = (n[:, None] * n[None, :] % SIDE) * (2.0 * np.pi / SIDE)
    factor = 1.0 / np.sqrt(SIDE)
    return (
        (np.cos(angles) * factor).astype(jnp.bfloat16),
        (-np.sin(angles) * factor).astype(jnp.bfloat16),
    )


def real_form(xp, re, im):
    return xp.concatenate(
        [xp.concatenate([re, -im], axis=1), xp.concatenate([im, re], axis=1)], axis=0
    )


def as_lines(block):
    rows = block.shape[0]
    lines = block.reshape(rows, 2, BLOCKS, LANES).transpose(0, 2, 1, 3)
    return lines.reshape(rows * 2 * BLOCKS, LANES)


def from_lines(lines):
    rows = lines.shape[0] // (2 * BLOCKS)
    block = lines.reshape(rows, BLOCKS, 2, LANES).transpose(0, 2, 1, 3)
    return block.reshape(rows, 2, LW)


def planes_kernel(lines_ref, planes_ref):
    for block in range(BLOCKS):
        for part in range(2):
            cells = lines_ref[pl.ds(2 * block + part, M, stride=2 * BLOCKS), :]
            planes_ref[part, :, block * LANES : (block + 1) * LANES] = cells.astype(
                jnp.bfloat16
            )


def split_planes(lines):
    return pl.pallas_call(
        planes_kernel,
        out_shape=jax.ShapeDtypeStruct((2, M, LW), jnp.bfloat16),
        in_specs=[pl.BlockSpec(memory_space=pltpu.VMEM)],
        out_specs=pl.BlockSpec(memory_space=pltpu.VMEM),
        compiler_params=pltpu.CompilerParams(vmem_limit_bytes=16 * MIB),
        name="split_planes",
    )(lines)


def total_kernel(inner_ref, other_ref, above_ref, below_ref, lines_ref):
    for block in range(BLOCKS):
        cols = slice(block * LANES, (block + 1) * LANES)
        for part in range(2):
            cells = inner_ref[part, :, cols] + other_ref[part, :, cols].astype(jnp.float32)
            cells = cells + below_ref[part, :, cols].astype(jnp.float32)
            cells = cells + above_ref[part, :, cols].astype(jnp.float32)
            lines_ref[pl.ds(2 * block + part, M, stride=2 * BLOCKS), :] = cells


def add_up(inner, other, above, below):
    return pl.pallas_call(
        total_kernel,
        out_shape=jax.ShapeDtypeStruct((M * 2 * BLOCKS, LANES), jnp.float32),
        in_specs=[pl.BlockSpec(memory_space=pltpu.VMEM)] * 4,
        out_specs=pl.BlockSpec(memory_space=pltpu.VMEM),
        compiler_params=pltpu.CompilerParams(vmem_limit_bytes=32 * MIB),
        name="add_up",
    )(inner, other, above, below)


def product(a_re, a_im, b_re, b_im):
    return a_re * b_re - a_im * b_im, a_re * b_im + a_im * b_re


def conj_product(a_re, a_im, b_re, b_im):
    return a_re * b_re + a_im * b_im, a_re * b_im - a_im * b_re


def transform(left, right, wave_re, wave_im):
    stacked = jnp.concatenate([wave_re, wave_im], axis=0).astype(jnp.bfloat16)
    middle = jnp.dot(left, stacked, preferred_element_type=jnp.float32)
    middle = middle.astype(jnp.bfloat16)
    middle = jnp.concatenate([middle[:SIDE], middle[SIDE:]], axis=1)
    result = jnp.dot(middle, right, preferred_element_type=jnp.float32)
    return result[:, :SIDE], result[:, SIDE:]


def rounded(wave):
    return tuple(plane.astype(jnp.bfloat16).astype(jnp.float32) for plane in wave)


def probes_kernel(
    section_ref,
    places_ref,
    counts_ref,
    own_ref,
    own_o_ref,
    low_ref,
    low_o_ref,
    up_ref,
    up_o_ref,
    observed_ref,
    probe_ref,
    prop_ref,
    prop_t_ref,
    dft_ref,
    dft_t_ref,
    inner_out,
    inner_o_out,
    low_out,
    low_o_out,
    up_out,
    up_o_out,
    ext,
    observed,
    window,
    totals,
    rims,
    psi1,
    in_sems,
    out_sems,
):
    mine = section_ref[0]
    other = 1 - mine
    loads = [
        pltpu.make_async_copy(source, ext.at[slice_no, part], in_sems.at[k])
        for k, (source, slice_no, part) in enumerate(
            (
                (own_ref, mine, 1),
                (own_o_ref, other, 1),
                (low_ref, mine, 0),
                (low_o_ref, other, 0),
                (up_ref, mine, 2),
                (up_o_ref, other, 2),
            )
        )
    ]
    loads.append(pltpu.make_async_copy(observed_ref.at[mine], observed, in_sems.at[6]))
    for load in loads:
        load.start()
    totals[...] = jnp.zeros_like(totals)
    for load in loads:
        load.wait()

    rim_row = lax.broadcasted_iota(jnp.int32, (M, WIDE), 0)
    lane_of_rim = lax.broadcasted_iota(jnp.int32, (M, LANES), 1)
    lane = lax.broadcasted_iota(jnp.int32, (SIDE + GROUP, LANES), 1)
    line = lax.broadcasted_iota(jnp.int32, (SIDE // GROUP, GROUP, SIDE), 1)
    line_out = lax.broadcasted_iota(jnp.int32, (1, GROUP, SIDE), 1)
    probe_re = probe_ref[0].astype(jnp.float32)
    probe_im = probe_ref[1].astype(jnp.float32)

    for slot in range(CAP):
        row = places_ref[mine * CAP + slot, 0]
        col = places_ref[mine * CAP + slot, 1]
        base = pl.multiple_of(jnp.minimum(col // LANES, BLOCKS - 3) * LANES, LANES)
        offset = col - base
        back = lax.rem(LANES - offset, LANES)
        forth = lax.rem(offset, LANES)
        row_base = pl.multiple_of(jnp.minimum(row // GROUP, M // GROUP - 1) * GROUP, GROUP)
        row_offset = row - row_base
        row_back = lax.rem(GROUP - row_offset, GROUP)
        row_forth = lax.rem(row_offset, GROUP)

        def to_left(cells):
            turned = [
                pltpu.roll(cells[:, k * LANES : (k + 1) * LANES], back, 1) for k in range(3)
            ]
            keep = lane_of_rim < LANES - offset
            return [jnp.where(keep, turned[k], turned[k + 1]) for k in range(2)]

        def cut(slice_no, part):
            cols = pl.ds(base, WIDE)
            rim = jnp.where(
                rim_row >= row,
                ext[slice_no, 0, part, :, cols].astype(jnp.float32),
                ext[slice_no, 2, part, :, cols].astype(jnp.float32),
            )
            rim = to_left(rim)
            middle = to_left(ext[slice_no, 1, part, :, cols].astype(jnp.float32))
            for k in range(2):
                here = slice(k * LANES, (k + 1) * LANES)
                window[slice_no, part, 0:M, here] = rim[k]
                window[slice_no, part, M : 2 * M, here] = middle[k]
                window[slice_no, part, 2 * M : 3 * M, here] = rim[k]

        def load_plane(slice_no, part):
            cells = window[slice_no, part, pl.ds(row_base, SIDE + GROUP), :]
            cells = pltpu.roll(cells.reshape(SIDE // GROUP + 1, GROUP, SIDE), row_back, 1)
            cells = jnp.where(line < GROUP - row_offset, cells[:-1], cells[1:])
            return cells.reshape(SIDE, SIDE)

        def load_window(slice_no):
            return load_plane(slice_no, 0), load_plane(slice_no, 1)

        def add_patch(slice_no, patch):
            for part in range(2):
                cells = pltpu.roll(patch[part].reshape(SIDE // GROUP, GROUP, SIDE), row_forth, 1)
                late = line_out >= row_offset
                cells = jnp.concatenate(
                    [
                        jnp.where(late, cells[:1], 0.0),
                        jnp.where(line[1:] >= row_offset, cells[1:], cells[:-1]),
                        jnp.where(late, 0.0, cells[-1:]),
                    ],
                    axis=0,
                ).reshape(SIDE + GROUP, SIDE)
                turned = [
                    pltpu.roll(cells[:, k * LANES : (k + 1) * LANES], forth, 1) for k in range(2)
                ]
                late = lane >= offset
                spread = jnp.concatenate(
                    [
                        jnp.where(late, turned[0], 0.0),
                        jnp.where(late, turned[1], turned[0]),
                        jnp.where(late, 0.0, turned[1]),
                    ],
                    axis=1,
                )
                totals[slice_no, part, pl.ds(row_base, SIDE + GROUP), pl.ds(base, WIDE)] += spread

        for slice_no in range(2):
            for part in range(2):
                cut(slice_no, part)

        phi = product(probe_re, probe_im, *load_window(0))
        wave = transform(prop_ref[...], prop_t_ref[...], *phi)
        psi1[0] = wave[0].astype(jnp.bfloat16)
        psi1[1] = wave[1].astype(jnp.bfloat16)
        phi = product(*rounded(wave), *load_window(1))
        far_re, far_im = transform(dft_ref[...], dft_t_ref[...], *phi)
        live = (slot < counts_ref[mine]).astype(jnp.float32)
        misfit = live * (far_re * far_re + far_im * far_im - observed[slot])
        spread = rounded(
            transform(dft_t_ref[...], dft_ref[...], misfit * far_re, misfit * far_im)
        )
        entering = (psi1[0].astype(jnp.float32), psi1[1].astype(jnp.float32))
        add_patch(1, conj_product(*entering, *spread))
        incoming = conj_product(*load_window(1), *spread)
        spread = rounded(transform(prop_t_ref[...], prop_ref[...], *incoming))
        add_patch(0, conj_product(probe_re, probe_im, *spread))

    stores = []

    def send(k, slice_no, first_row, target):
        rims[k] = totals[slice_no, :, first_row : first_row + M, :].astype(jnp.bfloat16)
        store = pltpu.make_async_copy(rims.at[k], target, out_sems.at[k])
        store.start()
        stores.append(store)

    send(0, other, 0, low_o_out)
    send(1, other, 2 * M, up_o_out)
    send(2, mine, 0, low_out)
    send(3, mine, 2 * M, up_out)
    send(4, other, M, inner_o_out)
    store = pltpu.make_async_copy(
        totals.at[mine, :, pl.ds(M, M), :], inner_out, out_sems.at[5]
    )
    store.start()
    stores.append(store)
    for store in stores:
        store.wait()


def probes(section, places, counts, planes, observed, probe, matrices):
    smem = pl.BlockSpec(memory_space=pltpu.SMEM)
    vmem = pl.BlockSpec(memory_space=pltpu.VMEM)
    apart = pl.BlockSpec(memory_space=pl.ANY)
    rim = jax.ShapeDtypeStruct((2, M, LW), jnp.bfloat16)
    return pl.pallas_call(
        probes_kernel,
        out_shape=[jax.ShapeDtypeStruct((2, M, LW), jnp.float32)] + [rim] * 5,
        in_specs=[smem] * 3 + [apart] * 7 + [vmem] * 5,
        out_specs=[apart] * 6,
        scratch_shapes=[
            pltpu.VMEM((2, 3, 2, M, LW), jnp.bfloat16),
            pltpu.VMEM((CAP, SIDE, SIDE), jnp.float32),
            pltpu.VMEM((2, 2, 3 * M, SIDE), jnp.float32),
            pltpu.VMEM((2, 2, 3 * M, LW), jnp.float32),
            pltpu.VMEM((5, 2, M, LW), jnp.bfloat16),
            pltpu.VMEM((2, SIDE, SIDE), jnp.bfloat16),
            pltpu.SemaphoreType.DMA((7,)),
            pltpu.SemaphoreType.DMA((6,)),
        ],
        compiler_params=pltpu.CompilerParams(vmem_limit_bytes=56 * MIB),
        name="probes",
    )(section, places, counts, *planes, observed, probe, *matrices)


def moved(value, steps):
    count = lax.axis_size("tile")
    first, last = (max(0, -steps), min(count, count - steps))
    return lax.ppermute(value, "tile", [(source, source + steps) for source in range(first, last)])


def across(value):
    return lax.ppermute(value, "depth", [(0, 1), (1, 0)])


def local(object_layer_slices, probe_wave, propagator, positions, counts, measured):
    own = split_planes(as_lines(object_layer_slices[0]))
    low = moved(own, 1)
    up = moved(own, -1)
    own_o = across(own)
    low_o = across(low)
    up_o = across(up)

    section = lax.axis_index("depth").astype(jnp.int32).reshape(1)
    probe = jnp.stack([probe_wave[:, 0], probe_wave[:, 1]])
    prop = real_form(jnp, propagator[:, 0], propagator[:, 1])
    dft = real_form(np, *dft_planes())
    matrices = (prop, prop.T, jnp.asarray(dft), jnp.asarray(dft.T.copy()))
    inner, inner_o, low_g, low_og, up_g, up_og = probes(
        section,
        positions.reshape(2 * CAP, 2),
        counts.reshape(2),
        (own, own_o, low, low_o, up, up_o),
        measured[0],
        probe,
        matrices,
    )
    above = moved(low_g + across(low_og), -1)
    below = moved(up_g + across(up_og), 1)
    lines = add_up(inner, across(inner_o), above, below)
    return from_lines(lines)[None]


def solution(mesh):
    placed = (
        P("depth", "tile", None, None),
        P(),
        P(),
        P("tile", None, None, None),
        P("tile", None),
        P("tile", None, None, None, None),
    )
    return jax.shard_map(
        local, mesh=mesh, in_specs=placed, out_specs=P("depth", "tile", None, None), check_vma=False
    )
```

```python
import jax
import jax.numpy as jnp
import numpy as np
from jax import lax
from jax.experimental import pallas as pl
from jax.experimental.pallas import tpu as pltpu
from jax.sharding import PartitionSpec as P

SIDE = 256
M = 128
CAP = 5
LW = 2048
LANES = 128
WIDE = SIDE + LANES
BLOCKS = LW // LANES
GROUP = 8
MIB = 1024 * 1024


def dft_planes():
    n = np.arange(SIDE)
    angles = (n[:, None] * n[None, :] % SIDE) * (2.0 * np.pi / SIDE)
    factor = 1.0 / np.sqrt(SIDE)
    return (
        (np.cos(angles) * factor).astype(jnp.bfloat16),
        (-np.sin(angles) * factor).astype(jnp.bfloat16),
    )


def real_form(xp, re, im):
    return xp.concatenate(
        [xp.concatenate([re, -im], axis=1), xp.concatenate([im, re], axis=1)], axis=0
    )


def as_lines(block):
    rows = block.shape[0]
    lines = block.reshape(rows, 2, BLOCKS, LANES).transpose(0, 2, 1, 3)
    return lines.reshape(rows, 2 * BLOCKS, LANES)


def from_lines(lines):
    rows = lines.shape[0]
    block = lines.reshape(rows, BLOCKS, 2, LANES).transpose(0, 2, 1, 3)
    return block.reshape(rows, 2, LW)


LINES = 2 * BLOCKS
PITCH = LINES + GROUP
STEPS = 4
ROWS = M // STEPS


def planes_kernel(lines_ref, planes_ref, held, sems):
    copies = [
        pltpu.make_async_copy(
            lines_ref.at[pl.ds(step * ROWS, ROWS)],
            held.reshape(M, PITCH, LANES).at[pl.ds(step * ROWS, ROWS), pl.ds(0, LINES), :],
            sems.at[step],
        )
        for step in range(STEPS)
    ]
    for copy in copies:
        copy.start()
    for step, copy in enumerate(copies):
        copy.wait()
        rows = slice(step * ROWS, (step + 1) * ROWS)
        for block in range(BLOCKS):
            for part in range(2):
                first = step * ROWS * PITCH + 2 * block + part
                cells = held[pl.ds(first, ROWS, stride=PITCH), :]
                planes_ref[part, rows, block * LANES : (block + 1) * LANES] = cells.astype(
                    jnp.bfloat16
                )


def split_planes(lines):
    return pl.pallas_call(
        planes_kernel,
        out_shape=jax.ShapeDtypeStruct((2, M, LW), jnp.bfloat16),
        in_specs=[pl.BlockSpec(memory_space=pltpu.HBM)],
        out_specs=pl.BlockSpec(memory_space=pltpu.VMEM),
        scratch_shapes=[
            pltpu.VMEM((M * PITCH, LANES), jnp.float32),
            pltpu.SemaphoreType.DMA((STEPS,)),
        ],
        compiler_params=pltpu.CompilerParams(vmem_limit_bytes=8 * MIB),
        name="split_planes",
    )(lines)


def total_kernel(inner_ref, far_ref, lines_ref, held, sems):
    copies = [
        pltpu.make_async_copy(
            held.reshape(M, PITCH, LANES).at[pl.ds(step * ROWS, ROWS), pl.ds(0, LINES), :],
            lines_ref.at[pl.ds(step * ROWS, ROWS)],
            sems.at[step],
        )
        for step in range(STEPS)
    ]
    for step, copy in enumerate(copies):
        rows = slice(step * ROWS, (step + 1) * ROWS)
        for block in range(BLOCKS):
            cols = slice(block * LANES, (block + 1) * LANES)
            for part in range(2):
                cells = inner_ref[part, rows, cols] + far_ref[part, rows, cols].astype(jnp.float32)
                first = step * ROWS * PITCH + 2 * block + part
                held[pl.ds(first, ROWS, stride=PITCH), :] = cells
        copy.start()
    for copy in copies:
        copy.wait()


def add_up(inner, far):
    return pl.pallas_call(
        total_kernel,
        out_shape=jax.ShapeDtypeStruct((M, LINES, LANES), jnp.float32),
        in_specs=[pl.BlockSpec(memory_space=pltpu.VMEM)] * 2,
        out_specs=pl.BlockSpec(memory_space=pltpu.HBM),
        scratch_shapes=[
            pltpu.VMEM((M * PITCH, LANES), jnp.float32),
            pltpu.SemaphoreType.DMA((STEPS,)),
        ],
        compiler_params=pltpu.CompilerParams(vmem_limit_bytes=12 * MIB),
        name="add_up",
    )(inner, far)


def product(a_re, a_im, b_re, b_im):
    return a_re * b_re - a_im * b_im, a_re * b_im + a_im * b_re


def conj_product(a_re, a_im, b_re, b_im):
    return a_re * b_re + a_im * b_im, a_re * b_im - a_im * b_re


def lanes(cells, count):
    return [cells[..., k * LANES : (k + 1) * LANES] for k in range(count)]


def wide(value):
    return value.astype(jnp.float32)


def probes_kernel(
    device_ref,
    places_ref,
    counts_ref,
    own_ref,
    own_o_ref,
    near_ref,
    near_o_ref,
    far_ref,
    far_o_ref,
    observed_ref,
    probe_ref,
    prop_hbm,
    dft_hbm,
    inner_out,
    inner_o_out,
    near_out,
    near_o_out,
    far_out,
    far_o_out,
    cuts,
    observed,
    window,
    object_1,
    psi_1,
    columns,
    rows,
    totals,
    matrices,
    cut_sems,
    observed_sem,
    matrix_sems,
):
    mine = device_ref[0]
    other = 1 - mine
    odd = device_ref[1]
    near_part, far_part = 2 - 2 * odd, 2 * odd

    def place(slot):
        row = places_ref[mine * CAP + slot, 0]
        col = places_ref[mine * CAP + slot, 1]
        base = pl.multiple_of(jnp.minimum(col // LANES, BLOCKS - 3) * LANES, LANES)
        row_base = pl.multiple_of(jnp.minimum(row // GROUP, M // GROUP - 1) * GROUP, GROUP)
        return row, row_base, row - row_base, base, col - base

    places = [place(slot) for slot in range(CAP)]

    def cut_copies(which, slot):
        base = places[slot][3]
        sources = ((near_ref, own_ref, far_ref), (near_o_ref, own_o_ref, far_o_ref))[which]
        return [
            pltpu.make_async_copy(
                source.at[:, :, pl.ds(base, WIDE)],
                cuts.at[(mine, other)[which], slot, part],
                cut_sems.at[which, slot, k],
            )
            for k, (part, source) in enumerate(zip((near_part, 1, far_part), sources))
        ]

    matrix_copies = [
        pltpu.make_async_copy(source, matrices.at[k], matrix_sems.at[k])
        for k, source in enumerate((prop_hbm, dft_hbm))
    ]
    for slot in range(CAP):
        for which in range(2):
            for copy in cut_copies(which, slot):
                copy.start()
        if slot == 0:
            matrix_copies[0].start()
    matrix_copies[1].start()
    prop_ref, prop_t_ref = matrices.at[0, 0], matrices.at[0, 1]
    dft_ref, dft_t_ref = matrices.at[1, 0], matrices.at[1, 1]
    observed_copy = pltpu.make_async_copy(observed_ref.at[mine], observed, observed_sem)
    observed_copy.start()
    totals[...] = jnp.zeros_like(totals)

    rim_row = lax.broadcasted_iota(jnp.int32, (M, WIDE), 0)
    lane_of_rim = lax.broadcasted_iota(jnp.int32, (M, LANES), 1)
    lane = lax.broadcasted_iota(jnp.int32, (SIDE + GROUP, LANES), 1)
    line = lax.broadcasted_iota(jnp.int32, (SIDE // GROUP, GROUP, SIDE), 1)
    line_out = lax.broadcasted_iota(jnp.int32, (1, GROUP, SIDE), 1)

    def cut(slice_no, slot, part):
        row, row_base, row_offset, _, offset = places[slot]
        back = lax.rem(LANES - offset, LANES)
        row_back = lax.rem(GROUP - row_offset, GROUP)
        keep = lane_of_rim < LANES - offset
        held = window.at[slot % 2, part]

        def to_left(cells):
            turned = [pltpu.roll(block, back, 1) for block in lanes(cells, 3)]
            return [jnp.where(keep, turned[k], turned[k + 1]) for k in range(2)]

        rim = to_left(
            jnp.where(
                rim_row >= row,
                wide(cuts[slice_no, slot, 0, part]),
                wide(cuts[slice_no, slot, 2, part]),
            )
        )
        middle = to_left(wide(cuts[slice_no, slot, 1, part]))
        for k in range(2):
            here = slice(k * LANES, (k + 1) * LANES)
            held[0:M, here] = rim[k]
            held[M : 2 * M, here] = middle[k]
            held[2 * M : 3 * M, here] = rim[k]
        cells = held[pl.ds(row_base, SIDE + GROUP), :].reshape(SIDE // GROUP + 1, GROUP, SIDE)
        cells = pltpu.roll(cells, row_back, 1)
        cells = jnp.where(line < GROUP - row_offset, cells[:-1], cells[1:])
        return cells.reshape(SIDE, SIDE)

    def add_patch(slice_no, slot, patch):
        _, row_base, row_offset, base, offset = places[slot]
        row_forth = lax.rem(row_offset, GROUP)
        forth = lax.rem(offset, LANES)
        for part in range(2):
            cells = pltpu.roll(patch[part].reshape(SIDE // GROUP, GROUP, SIDE), row_forth, 1)
            late = line_out >= row_offset
            cells = jnp.concatenate(
                [
                    jnp.where(late, cells[:1], 0.0),
                    jnp.where(line[1:] >= row_offset, cells[1:], cells[:-1]),
                    jnp.where(late, 0.0, cells[-1:]),
                ],
                axis=0,
            ).reshape(SIDE + GROUP, SIDE)
            turned = [pltpu.roll(block, forth, 1) for block in lanes(cells, 2)]
            late = lane >= offset
            spread = jnp.concatenate(
                [
                    jnp.where(late, turned[0], 0.0),
                    jnp.where(late, turned[1], turned[0]),
                    jnp.where(late, 0.0, turned[1]),
                ],
                axis=1,
            )
            totals[slice_no, part, pl.ds(row_base, SIDE + GROUP), pl.ds(base, WIDE)] += spread

    def to_columns(slot, wave, matrix):
        for part in range(2):
            columns[slot, part * SIDE : (part + 1) * SIDE, :] = wave[part].astype(jnp.bfloat16)
        middle = jnp.dot(matrix[...], columns[slot], preferred_element_type=jnp.float32)
        for part in range(2):
            rows[slot, :, part * SIDE : (part + 1) * SIDE] = middle[
                part * SIDE : (part + 1) * SIDE
            ].astype(jnp.bfloat16)

    def from_rows(slot, matrix):
        result = jnp.dot(rows[slot], matrix[...], preferred_element_type=jnp.float32)
        return result[:, :SIDE], result[:, SIDE:]

    def rounded(wave):
        return tuple(wide(plane.astype(jnp.bfloat16)) for plane in wave)

    def psi_0():
        return wide(probe_ref[0]), wide(probe_ref[1])

    def held_pair(ref, slot):
        return wide(ref[slot, 0]), wide(ref[slot, 1])

    for slot in range(CAP):
        for which in range(2):
            for copy in cut_copies(which, slot):
                copy.wait()
        phi = product(*psi_0(), cut(0, slot, 0), cut(0, slot, 1))
        if slot == 0:
            matrix_copies[0].wait()
        to_columns(slot, phi, prop_ref)
    matrix_copies[1].wait()
    for slot in range(CAP):
        for part in range(2):
            object_1[slot, part] = cut(1, slot, part).astype(jnp.bfloat16)
        wave = from_rows(slot, prop_t_ref)
        for part in range(2):
            psi_1[slot, part] = wave[part].astype(jnp.bfloat16)
        phi = product(*rounded(wave), *held_pair(object_1, slot))
        to_columns(slot, phi, dft_ref)
    observed_copy.wait()
    for slot in range(CAP):
        far_re, far_im = from_rows(slot, dft_t_ref)
        live = (slot < counts_ref[mine]).astype(jnp.float32)
        misfit = live * (far_re * far_re + far_im * far_im - observed[slot])
        to_columns(slot, (misfit * far_re, misfit * far_im), dft_t_ref)
    for slot in range(CAP):
        spread = rounded(from_rows(slot, dft_ref))
        to_columns(slot, conj_product(*held_pair(object_1, slot), *spread), prop_t_ref)
        add_patch(1, slot, conj_product(*held_pair(psi_1, slot), *spread))
    for slot in range(CAP):
        spread = rounded(from_rows(slot, prop_ref))
        add_patch(0, slot, conj_product(*psi_0(), *spread))

    def narrow(slice_no, first_row):
        return totals[slice_no, :, pl.ds(first_row, M), :].astype(jnp.bfloat16)

    near_row = pl.multiple_of(near_part * M, M)
    far_row = pl.multiple_of(far_part * M, M)
    far_o_out[...] = narrow(other, far_row)
    near_o_out[...] = narrow(other, near_row)
    far_out[...] = narrow(mine, far_row)
    near_out[...] = narrow(mine, near_row)
    inner_o_out[...] = narrow(other, M)
    inner_out[...] = totals[mine, :, M : 2 * M, :]


def probes(device, places, counts, planes, observed, probe, prop, dft):
    smem = pl.BlockSpec(memory_space=pltpu.SMEM)
    vmem = pl.BlockSpec(memory_space=pltpu.VMEM)
    apart = pl.BlockSpec(memory_space=pl.ANY)
    rim = jax.ShapeDtypeStruct((2, M, LW), jnp.bfloat16)
    return pl.pallas_call(
        probes_kernel,
        out_shape=[jax.ShapeDtypeStruct((2, M, LW), jnp.float32)] + [rim] * 5,
        in_specs=[smem] * 3 + [vmem] * 6 + [apart, vmem, apart, apart],
        out_specs=[vmem] * 6,
        scratch_shapes=[
            pltpu.VMEM((2, CAP, 3, 2, M, WIDE), jnp.bfloat16),
            pltpu.VMEM((CAP, SIDE, SIDE), jnp.float32),
            pltpu.VMEM((2, 2, 3 * M, SIDE), jnp.float32),
            pltpu.VMEM((CAP, 2, SIDE, SIDE), jnp.bfloat16),
            pltpu.VMEM((CAP, 2, SIDE, SIDE), jnp.bfloat16),
            pltpu.VMEM((CAP, 2 * SIDE, SIDE), jnp.bfloat16),
            pltpu.VMEM((CAP, SIDE, 2 * SIDE), jnp.bfloat16),
            pltpu.VMEM((2, 2, 3 * M, LW), jnp.float32),
            pltpu.VMEM((2, 2, 2 * SIDE, 2 * SIDE), jnp.bfloat16),
            pltpu.SemaphoreType.DMA((2, CAP, 3)),
            pltpu.SemaphoreType.DMA,
            pltpu.SemaphoreType.DMA((2,)),
        ],
        compiler_params=pltpu.CompilerParams(vmem_limit_bytes=38 * MIB),
        name="probes",
    )(device, places, counts, *planes, observed, probe, prop, dft)


def swap_near(value):
    count = lax.axis_size("tile")
    return lax.ppermute(value, "tile", [(t, t ^ 1) for t in range(count)])


def swap_far(value):
    count = lax.axis_size("tile")
    pairs = [(t, t + 1) for t in range(1, count - 1, 2)]
    return lax.ppermute(value, "tile", pairs + [(b, a) for a, b in pairs])


def across(value):
    return lax.ppermute(value, "depth", [(0, 1), (1, 0)])


def local(object_layer_slices, probe_wave, propagator, positions, counts, measured):
    lines = pltpu.with_memory_space_constraint(as_lines(object_layer_slices[0]), pltpu.HBM)
    own = split_planes(lines)
    near = swap_near(own)
    far = swap_far(own)
    own_o = across(own)

    device = jnp.stack([lax.axis_index("depth"), lax.axis_index("tile") % 2]).astype(jnp.int32)
    probe = jnp.stack([probe_wave[:, 0], probe_wave[:, 1]])
    prop = real_form(jnp, propagator[:, 0], propagator[:, 1])
    prop = jnp.stack([prop, prop.T])
    dft = real_form(np, *dft_planes())
    dft = jnp.asarray(np.stack([dft, dft.T]))
    near, probe, prop, places, live, device = lax.optimization_barrier(
        (near, probe, prop, positions.reshape(2 * CAP, 2), counts.reshape(2), device)
    )
    near_o = across(near)
    far_o = across(far)
    inner, inner_o, near_g, near_og, far_g, far_og = probes(
        device, places, live, (own, own_o, near, near_o, far, far_o), measured[0], probe, prop, dft
    )
    far_og = across(far_og)
    near_og = across(near_og)
    far_og, near_og, inner_o = lax.optimization_barrier((far_og, near_og, inner_o))
    far = swap_far(far_g + far_og)
    near = swap_near(near_g + near_og)
    inner = inner + across(inner_o).astype(jnp.float32)
    inner = inner + near.astype(jnp.float32)
    inner, far = lax.optimization_barrier((inner, far))
    return from_lines(add_up(inner, far))[None]


def solution(mesh):
    placed = (
        P("depth", "tile", None, None),
        P(),
        P(),
        P("tile", None, None, None),
        P("tile", None),
        P("tile", None, None, None, None),
    )
    return jax.shard_map(
        local, mesh=mesh, in_specs=placed, out_specs=P("depth", "tile", None, None), check_vma=False
    )
```

```python
import jax
import jax.numpy as jnp
import numpy as np
from jax import lax
from jax.experimental import pallas as pl
from jax.experimental.pallas import tpu as pltpu
from jax.sharding import PartitionSpec as P

SIDE = 256
M = 128
CAP = 5
LW = 2048
LANES = 128
WIDE = SIDE + LANES
BLOCKS = LW // LANES
GROUP = 8
MIB = 1024 * 1024


def dft_planes():
    n = np.arange(SIDE)
    angles = (n[:, None] * n[None, :] % SIDE) * (2.0 * np.pi / SIDE)
    factor = 1.0 / np.sqrt(SIDE)
    return (
        (np.cos(angles) * factor).astype(jnp.bfloat16),
        (-np.sin(angles) * factor).astype(jnp.bfloat16),
    )


def real_form(xp, re, im):
    return xp.concatenate(
        [xp.concatenate([re, -im], axis=1), xp.concatenate([im, re], axis=1)], axis=0
    )


def as_lines(block):
    rows = block.shape[0]
    lines = block.reshape(rows, 2, BLOCKS, LANES).transpose(0, 2, 1, 3)
    return lines.reshape(rows, 2 * BLOCKS, LANES)


def from_lines(lines):
    rows = lines.shape[0]
    block = lines.reshape(rows, BLOCKS, 2, LANES).transpose(0, 2, 1, 3)
    return block.reshape(rows, 2, LW)


LINES = 2 * BLOCKS
PITCH = LINES + GROUP
STEPS = 4
ROWS = M // STEPS


def planes_kernel(lines_ref, planes_ref, held, sems):
    copies = [
        pltpu.make_async_copy(
            lines_ref.at[pl.ds(step * ROWS, ROWS)],
            held.reshape(M, PITCH, LANES).at[pl.ds(step * ROWS, ROWS), pl.ds(0, LINES), :],
            sems.at[step],
        )
        for step in range(STEPS)
    ]
    for copy in copies:
        copy.start()
    for step, copy in enumerate(copies):
        copy.wait()
        rows = slice(step * ROWS, (step + 1) * ROWS)
        for block in range(BLOCKS):
            for part in range(2):
                first = step * ROWS * PITCH + 2 * block + part
                cells = held[pl.ds(first, ROWS, stride=PITCH), :]
                planes_ref[part, rows, block * LANES : (block + 1) * LANES] = cells.astype(
                    jnp.bfloat16
                )


def split_planes(lines):
    return pl.pallas_call(
        planes_kernel,
        out_shape=jax.ShapeDtypeStruct((2, M, LW), jnp.bfloat16),
        in_specs=[pl.BlockSpec(memory_space=pltpu.HBM)],
        out_specs=pl.BlockSpec(memory_space=pltpu.VMEM),
        scratch_shapes=[
            pltpu.VMEM((M * PITCH, LANES), jnp.float32),
            pltpu.SemaphoreType.DMA((STEPS,)),
        ],
        compiler_params=pltpu.CompilerParams(vmem_limit_bytes=8 * MIB),
        name="split_planes",
    )(lines)


def total_kernel(inner_ref, far_ref, lines_ref, held, sems):
    copies = [
        pltpu.make_async_copy(
            held.reshape(M, PITCH, LANES).at[pl.ds(step * ROWS, ROWS), pl.ds(0, LINES), :],
            lines_ref.at[pl.ds(step * ROWS, ROWS)],
            sems.at[step],
        )
        for step in range(STEPS)
    ]
    for step, copy in enumerate(copies):
        rows = slice(step * ROWS, (step + 1) * ROWS)
        for block in range(BLOCKS):
            cols = slice(block * LANES, (block + 1) * LANES)
            for part in range(2):
                cells = inner_ref[part, rows, cols] + far_ref[part, rows, cols].astype(jnp.float32)
                first = step * ROWS * PITCH + 2 * block + part
                held[pl.ds(first, ROWS, stride=PITCH), :] = cells
        copy.start()
    for copy in copies:
        copy.wait()


def add_up(inner, far):
    return pl.pallas_call(
        total_kernel,
        out_shape=jax.ShapeDtypeStruct((M, LINES, LANES), jnp.float32),
        in_specs=[pl.BlockSpec(memory_space=pltpu.VMEM)] * 2,
        out_specs=pl.BlockSpec(memory_space=pltpu.HBM),
        scratch_shapes=[
            pltpu.VMEM((M * PITCH, LANES), jnp.float32),
            pltpu.SemaphoreType.DMA((STEPS,)),
        ],
        compiler_params=pltpu.CompilerParams(vmem_limit_bytes=12 * MIB),
        name="add_up",
    )(inner, far)


def product(a_re, a_im, b_re, b_im):
    return a_re * b_re - a_im * b_im, a_re * b_im + a_im * b_re


def conj_product(a_re, a_im, b_re, b_im):
    return a_re * b_re + a_im * b_im, a_re * b_im - a_im * b_re


def lanes(cells, count):
    return [cells[..., k * LANES : (k + 1) * LANES] for k in range(count)]


def wide(value):
    return value.astype(jnp.float32)


def probes_kernel(
    device_ref,
    places_ref,
    counts_ref,
    own_ref,
    own_o_ref,
    near_ref,
    near_o_ref,
    far_ref,
    far_o_ref,
    observed_ref,
    probe_ref,
    prop_hbm,
    dft_hbm,
    inner_out,
    inner_o_out,
    near_out,
    near_o_out,
    far_out,
    far_o_out,
    cuts,
    observed,
    window,
    object_1,
    psi_1,
    columns,
    rows,
    totals,
    waves,
    matrices,
    cut_sems,
    observed_sem,
    matrix_sems,
):
    mine = device_ref[0]
    other = 1 - mine
    odd = device_ref[1]
    near_part, far_part = 2 - 2 * odd, 2 * odd

    def place(slot):
        row = places_ref[mine * CAP + slot, 0]
        col = places_ref[mine * CAP + slot, 1]
        base = pl.multiple_of(jnp.minimum(col // LANES, BLOCKS - 3) * LANES, LANES)
        row_base = pl.multiple_of(jnp.minimum(row // GROUP, M // GROUP - 1) * GROUP, GROUP)
        return row, row_base, row - row_base, base, col - base

    places = [place(slot) for slot in range(CAP)]

    def cut_copies(which, slot):
        base = places[slot][3]
        sources = ((near_ref, own_ref, far_ref), (near_o_ref, own_o_ref, far_o_ref))[which]
        return [
            pltpu.make_async_copy(
                source.at[:, :, pl.ds(base, WIDE)],
                cuts.at[(mine, other)[which], slot, part],
                cut_sems.at[which, slot, k],
            )
            for k, (part, source) in enumerate(zip((near_part, 1, far_part), sources))
        ]

    matrix_copies = [
        pltpu.make_async_copy(source, matrices.at[k], matrix_sems.at[k])
        for k, source in enumerate((prop_hbm, dft_hbm))
    ]
    for slot in range(CAP):
        for which in range(2):
            for copy in cut_copies(which, slot):
                copy.start()
        if slot == 0:
            matrix_copies[0].start()
    matrix_copies[1].start()
    prop_ref, prop_t_ref = matrices.at[0, 0], matrices.at[0, 1]
    dft_ref, dft_t_ref = matrices.at[1, 0], matrices.at[1, 1]
    observed_copy = pltpu.make_async_copy(observed_ref.at[mine], observed, observed_sem)
    observed_copy.start()
    totals[...] = jnp.zeros_like(totals)

    rim_row = lax.broadcasted_iota(jnp.int32, (M, WIDE), 0)
    lane_of_rim = lax.broadcasted_iota(jnp.int32, (M, LANES), 1)
    lane = lax.broadcasted_iota(jnp.int32, (SIDE + GROUP, LANES), 1)
    line = lax.broadcasted_iota(jnp.int32, (SIDE // GROUP, GROUP, SIDE), 1)
    line_out = lax.broadcasted_iota(jnp.int32, (1, GROUP, SIDE), 1)

    def cut(slice_no, slot, part):
        row, row_base, row_offset, _, offset = places[slot]
        back = lax.rem(LANES - offset, LANES)
        row_back = lax.rem(GROUP - row_offset, GROUP)
        keep = lane_of_rim < LANES - offset
        held = window.at[slot % 2, part]

        def to_left(cells):
            turned = [pltpu.roll(block, back, 1) for block in lanes(cells, 3)]
            return [jnp.where(keep, turned[k], turned[k + 1]) for k in range(2)]

        rim = to_left(
            jnp.where(
                rim_row >= row,
                wide(cuts[slice_no, slot, 0, part]),
                wide(cuts[slice_no, slot, 2, part]),
            )
        )
        middle = to_left(wide(cuts[slice_no, slot, 1, part]))
        for k in range(2):
            here = slice(k * LANES, (k + 1) * LANES)
            held[0:M, here] = rim[k]
            held[M : 2 * M, here] = middle[k]
            held[2 * M : 3 * M, here] = rim[k]
        cells = held[pl.ds(row_base, SIDE + GROUP), :].reshape(SIDE // GROUP + 1, GROUP, SIDE)
        cells = pltpu.roll(cells, row_back, 1)
        cells = jnp.where(line < GROUP - row_offset, cells[:-1], cells[1:])
        return cells.reshape(SIDE, SIDE)

    def add_patch(slice_no, slot, patch):
        _, row_base, row_offset, base, offset = places[slot]
        row_forth = lax.rem(row_offset, GROUP)
        forth = lax.rem(offset, LANES)
        for part in range(2):
            cells = pltpu.roll(patch[part].reshape(SIDE // GROUP, GROUP, SIDE), row_forth, 1)
            late = line_out >= row_offset
            cells = jnp.concatenate(
                [
                    jnp.where(late, cells[:1], 0.0),
                    jnp.where(line[1:] >= row_offset, cells[1:], cells[:-1]),
                    jnp.where(late, 0.0, cells[-1:]),
                ],
                axis=0,
            ).reshape(SIDE + GROUP, SIDE)
            turned = [pltpu.roll(block, forth, 1) for block in lanes(cells, 2)]
            late = lane >= offset
            spread = jnp.concatenate(
                [
                    jnp.where(late, turned[0], 0.0),
                    jnp.where(late, turned[1], turned[0]),
                    jnp.where(late, 0.0, turned[1]),
                ],
                axis=1,
            )
            totals[slice_no, part, pl.ds(row_base, SIDE + GROUP), pl.ds(base, WIDE)] += spread

    def to_columns(slot, wave, matrix):
        for part in range(2):
            columns[part * SIDE : (part + 1) * SIDE, slot * SIDE : (slot + 1) * SIDE] = wave[part].astype(jnp.bfloat16)
        if slot < CAP - 1:
            return
        middle = jnp.dot(matrix[...], columns[...], preferred_element_type=jnp.float32)
        for k in range(CAP):
            for part in range(2):
                rows[k, :, part * SIDE : (part + 1) * SIDE] = middle[
                    part * SIDE : (part + 1) * SIDE, k * SIDE : (k + 1) * SIDE
                ].astype(jnp.bfloat16)

    def all_rows(matrix):
        every = rows[...].reshape(CAP * SIDE, 2 * SIDE)
        result = jnp.dot(every, matrix[...], preferred_element_type=jnp.float32)
        waves[...] = result.reshape(CAP, SIDE, 2 * SIDE)

    def from_rows(slot):
        return waves[slot, :, :SIDE], waves[slot, :, SIDE:]

    def rounded(wave):
        return tuple(wide(plane.astype(jnp.bfloat16)) for plane in wave)

    def psi_0():
        return wide(probe_ref[0]), wide(probe_ref[1])

    def held_pair(ref, slot):
        return wide(ref[slot, 0]), wide(ref[slot, 1])

    for slot in range(CAP):
        for which in range(2):
            for copy in cut_copies(which, slot):
                copy.wait()
        phi = product(*psi_0(), cut(0, slot, 0), cut(0, slot, 1))
        if slot == 0:
            matrix_copies[0].wait()
        to_columns(slot, phi, prop_ref)
    matrix_copies[1].wait()
    all_rows(prop_t_ref)
    for slot in range(CAP):
        for part in range(2):
            object_1[slot, part] = cut(1, slot, part).astype(jnp.bfloat16)
        wave = from_rows(slot)
        for part in range(2):
            psi_1[slot, part] = wave[part].astype(jnp.bfloat16)
        phi = product(*rounded(wave), *held_pair(object_1, slot))
        to_columns(slot, phi, dft_ref)
    observed_copy.wait()
    all_rows(dft_t_ref)
    for slot in range(CAP):
        far_re, far_im = from_rows(slot)
        live = (slot < counts_ref[mine]).astype(jnp.float32)
        misfit = live * (far_re * far_re + far_im * far_im - observed[slot])
        to_columns(slot, (misfit * far_re, misfit * far_im), dft_t_ref)
    all_rows(dft_ref)
    for slot in range(CAP):
        spread = rounded(from_rows(slot))
        to_columns(slot, conj_product(*held_pair(object_1, slot), *spread), prop_t_ref)
        add_patch(1, slot, conj_product(*held_pair(psi_1, slot), *spread))
    all_rows(prop_ref)
    for slot in range(CAP):
        spread = rounded(from_rows(slot))
        add_patch(0, slot, conj_product(*psi_0(), *spread))

    def narrow(slice_no, first_row):
        return totals[slice_no, :, pl.ds(first_row, M), :].astype(jnp.bfloat16)

    near_row = pl.multiple_of(near_part * M, M)
    far_row = pl.multiple_of(far_part * M, M)
    far_o_out[...] = narrow(other, far_row)
    near_o_out[...] = narrow(other, near_row)
    far_out[...] = narrow(mine, far_row)
    near_out[...] = narrow(mine, near_row)
    inner_o_out[...] = narrow(other, M)
    inner_out[...] = totals[mine, :, M : 2 * M, :]


def probes(device, places, counts, planes, observed, probe, prop, dft):
    smem = pl.BlockSpec(memory_space=pltpu.SMEM)
    vmem = pl.BlockSpec(memory_space=pltpu.VMEM)
    apart = pl.BlockSpec(memory_space=pl.ANY)
    rim = jax.ShapeDtypeStruct((2, M, LW), jnp.bfloat16)
    return pl.pallas_call(
        probes_kernel,
        out_shape=[jax.ShapeDtypeStruct((2, M, LW), jnp.float32)] + [rim] * 5,
        in_specs=[smem] * 3 + [vmem] * 6 + [apart, vmem, apart, apart],
        out_specs=[vmem] * 6,
        scratch_shapes=[
            pltpu.VMEM((2, CAP, 3, 2, M, WIDE), jnp.bfloat16),
            pltpu.VMEM((CAP, SIDE, SIDE), jnp.float32),
            pltpu.VMEM((2, 2, 3 * M, SIDE), jnp.float32),
            pltpu.VMEM((CAP, 2, SIDE, SIDE), jnp.bfloat16),
            pltpu.VMEM((CAP, 2, SIDE, SIDE), jnp.bfloat16),
            pltpu.VMEM((2 * SIDE, CAP * SIDE), jnp.bfloat16),
            pltpu.VMEM((CAP, SIDE, 2 * SIDE), jnp.bfloat16),
            pltpu.VMEM((2, 2, 3 * M, LW), jnp.float32),
            pltpu.VMEM((CAP, SIDE, 2 * SIDE), jnp.float32),
            pltpu.VMEM((2, 2, 2 * SIDE, 2 * SIDE), jnp.bfloat16),
            pltpu.SemaphoreType.DMA((2, CAP, 3)),
            pltpu.SemaphoreType.DMA,
            pltpu.SemaphoreType.DMA((2,)),
        ],
        compiler_params=pltpu.CompilerParams(vmem_limit_bytes=38 * MIB),
        name="probes",
    )(device, places, counts, *planes, observed, probe, prop, dft)


def swap_near(value):
    count = lax.axis_size("tile")
    return lax.ppermute(value, "tile", [(t, t ^ 1) for t in range(count)])


def swap_far(value):
    count = lax.axis_size("tile")
    pairs = [(t, t + 1) for t in range(1, count - 1, 2)]
    return lax.ppermute(value, "tile", pairs + [(b, a) for a, b in pairs])


def across(value):
    return lax.ppermute(value, "depth", [(0, 1), (1, 0)])


def local(object_layer_slices, probe_wave, propagator, positions, counts, measured):
    lines = pltpu.with_memory_space_constraint(as_lines(object_layer_slices[0]), pltpu.HBM)
    own = split_planes(lines)
    near = swap_near(own)
    far = swap_far(own)
    own_o = across(own)

    device = jnp.stack([lax.axis_index("depth"), lax.axis_index("tile") % 2]).astype(jnp.int32)
    probe = jnp.stack([probe_wave[:, 0], probe_wave[:, 1]])
    prop = real_form(jnp, propagator[:, 0], propagator[:, 1])
    prop = jnp.stack([prop, prop.T])
    dft = real_form(np, *dft_planes())
    dft = jnp.asarray(np.stack([dft, dft.T]))
    near, probe, prop, places, live, device = lax.optimization_barrier(
        (near, probe, prop, positions.reshape(2 * CAP, 2), counts.reshape(2), device)
    )
    near_o = across(near)
    far_o = across(far)
    inner, inner_o, near_g, near_og, far_g, far_og = probes(
        device, places, live, (own, own_o, near, near_o, far, far_o), measured[0], probe, prop, dft
    )
    far_og = across(far_og)
    near_og = across(near_og)
    far_g = far_g + far_og
    far = swap_far(far_g)
    far_g, near_og, inner_o = lax.optimization_barrier((far_g, near_og, inner_o))
    near = swap_near(near_g + near_og)
    inner = inner + across(inner_o).astype(jnp.float32)
    inner = inner + far.astype(jnp.float32)
    inner, near = lax.optimization_barrier((inner, near))
    return from_lines(add_up(inner, near))[None]


def solution(mesh):
    placed = (
        P("depth", "tile", None, None),
        P(),
        P(),
        P("tile", None, None, None),
        P("tile", None),
        P("tile", None, None, None, None),
    )
    return jax.shard_map(
        local, mesh=mesh, in_specs=placed, out_specs=P("depth", "tile", None, None), check_vma=False
    )
```

```python
import jax
import jax.numpy as jnp
import numpy as np
from jax import lax
from jax.experimental import pallas as pl
from jax.experimental.pallas import tpu as pltpu
from jax.sharding import PartitionSpec as P

SIDE = 256
M = 128
CAP = 5
LW = 2048
LANES = 128
WIDE = SIDE + LANES
BLOCKS = LW // LANES
GROUP = 8
MIB = 1024 * 1024


def dft_planes():
    n = np.arange(SIDE)
    angles = (n[:, None] * n[None, :] % SIDE) * (2.0 * np.pi / SIDE)
    factor = 1.0 / np.sqrt(SIDE)
    return (
        (np.cos(angles) * factor).astype(jnp.bfloat16),
        (-np.sin(angles) * factor).astype(jnp.bfloat16),
    )


def real_form(xp, re, im):
    return xp.concatenate(
        [xp.concatenate([re, -im], axis=1), xp.concatenate([im, re], axis=1)], axis=0
    )


def as_lines(block):
    rows = block.shape[0]
    lines = block.reshape(rows, 2, BLOCKS, LANES).transpose(0, 2, 1, 3)
    return lines.reshape(rows, 2 * BLOCKS, LANES)


def from_lines(lines):
    rows = lines.shape[0]
    block = lines.reshape(rows, BLOCKS, 2, LANES).transpose(0, 2, 1, 3)
    return block.reshape(rows, 2, LW)


LINES = 2 * BLOCKS
PITCH = LINES + GROUP
STEPS = 4
ROWS = M // STEPS


def planes_kernel(lines_ref, planes_ref, held, sems):
    copies = [
        pltpu.make_async_copy(
            lines_ref.at[pl.ds(step * ROWS, ROWS)],
            held.reshape(M, PITCH, LANES).at[pl.ds(step * ROWS, ROWS), pl.ds(0, LINES), :],
            sems.at[step],
        )
        for step in range(STEPS)
    ]
    for copy in copies:
        copy.start()
    for step, copy in enumerate(copies):
        copy.wait()
        rows = slice(step * ROWS, (step + 1) * ROWS)
        for block in range(BLOCKS):
            for part in range(2):
                first = step * ROWS * PITCH + 2 * block + part
                cells = held[pl.ds(first, ROWS, stride=PITCH), :]
                planes_ref[part, rows, block * LANES : (block + 1) * LANES] = cells.astype(
                    jnp.bfloat16
                )


def split_planes(lines):
    return pl.pallas_call(
        planes_kernel,
        out_shape=jax.ShapeDtypeStruct((2, M, LW), jnp.bfloat16),
        in_specs=[pl.BlockSpec(memory_space=pltpu.HBM)],
        out_specs=pl.BlockSpec(memory_space=pltpu.VMEM),
        scratch_shapes=[
            pltpu.VMEM((M * PITCH, LANES), jnp.float32),
            pltpu.SemaphoreType.DMA((STEPS,)),
        ],
        compiler_params=pltpu.CompilerParams(vmem_limit_bytes=8 * MIB),
        name="split_planes",
    )(lines)


def total_kernel(inner_ref, far_ref, lines_ref, held, sems):
    copies = [
        pltpu.make_async_copy(
            held.reshape(M, PITCH, LANES).at[pl.ds(step * ROWS, ROWS), pl.ds(0, LINES), :],
            lines_ref.at[pl.ds(step * ROWS, ROWS)],
            sems.at[step],
        )
        for step in range(STEPS)
    ]
    for step, copy in enumerate(copies):
        rows = slice(step * ROWS, (step + 1) * ROWS)
        for block in range(BLOCKS):
            cols = slice(block * LANES, (block + 1) * LANES)
            for part in range(2):
                cells = inner_ref[part, rows, cols] + far_ref[part, rows, cols].astype(jnp.float32)
                first = step * ROWS * PITCH + 2 * block + part
                held[pl.ds(first, ROWS, stride=PITCH), :] = cells
        copy.start()
    for copy in copies:
        copy.wait()


def add_up(inner, far):
    return pl.pallas_call(
        total_kernel,
        out_shape=jax.ShapeDtypeStruct((M, LINES, LANES), jnp.float32),
        in_specs=[pl.BlockSpec(memory_space=pltpu.VMEM)] * 2,
        out_specs=pl.BlockSpec(memory_space=pltpu.HBM),
        scratch_shapes=[
            pltpu.VMEM((M * PITCH, LANES), jnp.float32),
            pltpu.SemaphoreType.DMA((STEPS,)),
        ],
        compiler_params=pltpu.CompilerParams(vmem_limit_bytes=12 * MIB),
        name="add_up",
    )(inner, far)


def product(a_re, a_im, b_re, b_im):
    return a_re * b_re - a_im * b_im, a_re * b_im + a_im * b_re


def conj_product(a_re, a_im, b_re, b_im):
    return a_re * b_re + a_im * b_im, a_re * b_im - a_im * b_re


def lanes(cells, count):
    return [cells[..., k * LANES : (k + 1) * LANES] for k in range(count)]


def wide(value):
    return value.astype(jnp.float32)


def probes_kernel(
    device_ref,
    places_ref,
    counts_ref,
    own_ref,
    own_o_ref,
    near_ref,
    near_o_ref,
    far_ref,
    far_o_ref,
    observed_ref,
    probe_ref,
    prop_hbm,
    dft_hbm,
    inner_out,
    inner_o_out,
    near_out,
    near_o_out,
    far_out,
    far_o_out,
    cuts,
    observed,
    window,
    object_1,
    psi_1,
    columns,
    rows,
    totals,
    matrices,
    cut_sems,
    observed_sem,
    matrix_sems,
):
    mine = device_ref[0]
    other = 1 - mine
    odd = device_ref[1]
    near_part, far_part = 2 - 2 * odd, 2 * odd

    def place(slot):
        row = places_ref[mine * CAP + slot, 0]
        col = places_ref[mine * CAP + slot, 1]
        base = pl.multiple_of(jnp.minimum(col // LANES, BLOCKS - 3) * LANES, LANES)
        row_base = pl.multiple_of(jnp.minimum(row // GROUP, M // GROUP - 1) * GROUP, GROUP)
        return row, row_base, row - row_base, base, col - base

    places = [place(slot) for slot in range(CAP)]

    def cut_copies(which, slot):
        base = places[slot][3]
        sources = ((near_ref, own_ref, far_ref), (near_o_ref, own_o_ref, far_o_ref))[which]
        return [
            pltpu.make_async_copy(
                source.at[:, :, pl.ds(base, WIDE)],
                cuts.at[(mine, other)[which], slot, part],
                cut_sems.at[which, slot, k],
            )
            for k, (part, source) in enumerate(zip((near_part, 1, far_part), sources))
        ]

    matrix_copies = [
        pltpu.make_async_copy(source, matrices.at[k], matrix_sems.at[k])
        for k, source in enumerate((prop_hbm, dft_hbm))
    ]
    for slot in range(CAP):
        for which in range(2):
            for copy in cut_copies(which, slot):
                copy.start()
        if slot == 0:
            matrix_copies[0].start()
    matrix_copies[1].start()
    prop_ref, prop_t_ref = matrices.at[0, 0], matrices.at[0, 1]
    dft_ref, dft_t_ref = matrices.at[1, 0], matrices.at[1, 1]
    observed_copy = pltpu.make_async_copy(observed_ref.at[mine], observed, observed_sem)
    observed_copy.start()
    totals[...] = jnp.zeros_like(totals)

    rim_row = lax.broadcasted_iota(jnp.int32, (M, WIDE), 0)
    lane_of_rim = lax.broadcasted_iota(jnp.int32, (M, LANES), 1)
    lane = lax.broadcasted_iota(jnp.int32, (SIDE + GROUP, LANES), 1)
    line = lax.broadcasted_iota(jnp.int32, (SIDE // GROUP, GROUP, SIDE), 1)
    line_out = lax.broadcasted_iota(jnp.int32, (1, GROUP, SIDE), 1)

    def cut(slice_no, slot, part):
        row, row_base, row_offset, _, offset = places[slot]
        back = lax.rem(LANES - offset, LANES)
        row_back = lax.rem(GROUP - row_offset, GROUP)
        keep = lane_of_rim < LANES - offset
        held = window.at[slot % 2, part]

        def to_left(cells):
            turned = [pltpu.roll(block, back, 1) for block in lanes(cells, 3)]
            return [jnp.where(keep, turned[k], turned[k + 1]) for k in range(2)]

        rim = to_left(
            wide(
                jnp.where(
                    rim_row >= row,
                    cuts[slice_no, slot, 0, part],
                    cuts[slice_no, slot, 2, part],
                )
            )
        )
        middle = to_left(wide(cuts[slice_no, slot, 1, part]))
        for k in range(2):
            here = slice(k * LANES, (k + 1) * LANES)
            held[0:M, here] = rim[k]
            held[M : 2 * M, here] = middle[k]
            held[2 * M : 3 * M, here] = rim[k]
        cells = held[pl.ds(row_base, SIDE + GROUP), :].reshape(SIDE // GROUP + 1, GROUP, SIDE)
        cells = pltpu.roll(cells, row_back, 1)
        cells = jnp.where(line < GROUP - row_offset, cells[:-1], cells[1:])
        return cells.reshape(SIDE, SIDE)

    def add_patch(slice_no, slot, patch):
        _, row_base, row_offset, base, offset = places[slot]
        row_forth = lax.rem(row_offset, GROUP)
        forth = lax.rem(offset, LANES)
        for part in range(2):
            cells = pltpu.roll(patch[part].reshape(SIDE // GROUP, GROUP, SIDE), row_forth, 1)
            late = line_out >= row_offset
            cells = jnp.concatenate(
                [
                    jnp.where(late, cells[:1], 0.0),
                    jnp.where(line[1:] >= row_offset, cells[1:], cells[:-1]),
                    jnp.where(late, 0.0, cells[-1:]),
                ],
                axis=0,
            ).reshape(SIDE + GROUP, SIDE)
            turned = [pltpu.roll(block, forth, 1) for block in lanes(cells, 2)]
            late = lane >= offset
            spread = jnp.concatenate(
                [
                    jnp.where(late, turned[0], 0.0),
                    jnp.where(late, turned[1], turned[0]),
                    jnp.where(late, 0.0, turned[1]),
                ],
                axis=1,
            )
            totals[slice_no, part, pl.ds(row_base, SIDE + GROUP), pl.ds(base, WIDE)] += spread

    def to_columns(slot, wave, matrix):
        for part in range(2):
            columns[part * SIDE : (part + 1) * SIDE, slot * SIDE : (slot + 1) * SIDE] = wave[part].astype(jnp.bfloat16)
        if slot < CAP - 1:
            return
        middle = jnp.dot(matrix[...], columns[...], preferred_element_type=jnp.float32)
        for k in range(CAP):
            for part in range(2):
                rows[k, :, part * SIDE : (part + 1) * SIDE] = middle[
                    part * SIDE : (part + 1) * SIDE, k * SIDE : (k + 1) * SIDE
                ].astype(jnp.bfloat16)

    def from_rows(slot, matrix):
        result = jnp.dot(rows[slot], matrix[...], preferred_element_type=jnp.float32)
        return result[:, :SIDE], result[:, SIDE:]

    def rounded(wave):
        return tuple(wide(plane.astype(jnp.bfloat16)) for plane in wave)

    def psi_0():
        return wide(probe_ref[0]), wide(probe_ref[1])

    def held_pair(ref, slot):
        return wide(ref[slot, 0]), wide(ref[slot, 1])

    for slot in range(CAP):
        for which in range(2):
            for copy in cut_copies(which, slot):
                copy.wait()
        phi = product(*psi_0(), cut(0, slot, 0), cut(0, slot, 1))
        if slot == 0:
            matrix_copies[0].wait()
        to_columns(slot, phi, prop_ref)
    matrix_copies[1].wait()
    for slot in range(CAP):
        for part in range(2):
            object_1[slot, part] = cut(1, slot, part).astype(jnp.bfloat16)
        wave = from_rows(slot, prop_t_ref)
        for part in range(2):
            psi_1[slot, part] = wave[part].astype(jnp.bfloat16)
        phi = product(*rounded(wave), *held_pair(object_1, slot))
        to_columns(slot, phi, dft_ref)
    observed_copy.wait()
    for slot in range(CAP):
        far_re, far_im = from_rows(slot, dft_t_ref)
        live = (slot < counts_ref[mine]).astype(jnp.float32)
        misfit = live * (far_re * far_re + far_im * far_im - observed[slot])
        to_columns(slot, (misfit * far_re, misfit * far_im), dft_t_ref)
    for slot in range(CAP):
        spread = rounded(from_rows(slot, dft_ref))
        to_columns(slot, conj_product(*held_pair(object_1, slot), *spread), prop_t_ref)
        add_patch(1, slot, conj_product(*held_pair(psi_1, slot), *spread))
    for slot in range(CAP):
        spread = rounded(from_rows(slot, prop_ref))
        add_patch(0, slot, conj_product(*psi_0(), *spread))

    def narrow(slice_no, first_row):
        return totals[slice_no, :, pl.ds(first_row, M), :].astype(jnp.bfloat16)

    near_row = pl.multiple_of(near_part * M, M)
    far_row = pl.multiple_of(far_part * M, M)
    far_o_out[...] = narrow(other, far_row)
    near_o_out[...] = narrow(other, near_row)
    far_out[...] = narrow(mine, far_row)
    near_out[...] = narrow(mine, near_row)
    inner_o_out[...] = narrow(other, M)
    inner_out[...] = totals[mine, :, M : 2 * M, :]


def probes(device, places, counts, planes, observed, probe, prop, dft):
    smem = pl.BlockSpec(memory_space=pltpu.SMEM)
    vmem = pl.BlockSpec(memory_space=pltpu.VMEM)
    apart = pl.BlockSpec(memory_space=pl.ANY)
    rim = jax.ShapeDtypeStruct((2, M, LW), jnp.bfloat16)
    return pl.pallas_call(
        probes_kernel,
        out_shape=[jax.ShapeDtypeStruct((2, M, LW), jnp.float32)] + [rim] * 5,
        in_specs=[smem] * 3 + [apart] * 7 + [vmem, apart, apart],
        out_specs=[vmem] * 6,
        scratch_shapes=[
            pltpu.VMEM((2, CAP, 3, 2, M, WIDE), jnp.bfloat16),
            pltpu.VMEM((CAP, SIDE, SIDE), jnp.float32),
            pltpu.VMEM((2, 2, 3 * M, SIDE), jnp.float32),
            pltpu.VMEM((CAP, 2, SIDE, SIDE), jnp.bfloat16),
            pltpu.VMEM((CAP, 2, SIDE, SIDE), jnp.bfloat16),
            pltpu.VMEM((2 * SIDE, CAP * SIDE), jnp.bfloat16),
            pltpu.VMEM((CAP, SIDE, 2 * SIDE), jnp.bfloat16),
            pltpu.VMEM((2, 2, 3 * M, LW), jnp.float32),
            pltpu.VMEM((2, 2, 2 * SIDE, 2 * SIDE), jnp.bfloat16),
            pltpu.SemaphoreType.DMA((2, CAP, 3)),
            pltpu.SemaphoreType.DMA,
            pltpu.SemaphoreType.DMA((2,)),
        ],
        compiler_params=pltpu.CompilerParams(vmem_limit_bytes=38 * MIB),
        name="probes",
    )(device, places, counts, *planes, observed, probe, prop, dft)


def swap_near(value):
    count = lax.axis_size("tile")
    return lax.ppermute(value, "tile", [(t, t ^ 1) for t in range(count)])


def swap_far(value):
    count = lax.axis_size("tile")
    pairs = [(t, t + 1) for t in range(1, count - 1, 2)]
    return lax.ppermute(value, "tile", pairs + [(b, a) for a, b in pairs])


def across(value):
    return lax.ppermute(value, "depth", [(0, 1), (1, 0)])


def local(object_layer_slices, probe_wave, propagator, positions, counts, measured):
    lines = pltpu.with_memory_space_constraint(as_lines(object_layer_slices[0]), pltpu.HBM)
    own = split_planes(lines)
    near = swap_near(own)
    far = swap_far(own)
    own_o = across(own)

    device = jnp.stack([lax.axis_index("depth"), lax.axis_index("tile") % 2]).astype(jnp.int32)
    probe = jnp.stack([probe_wave[:, 0], probe_wave[:, 1]])
    prop = real_form(jnp, propagator[:, 0], propagator[:, 1])
    prop = jnp.stack([prop, prop.T])
    dft = real_form(np, *dft_planes())
    dft = jnp.asarray(np.stack([dft, dft.T]))
    near, probe, prop, places, live, device = lax.optimization_barrier(
        (near, probe, prop, positions.reshape(2 * CAP, 2), counts.reshape(2), device)
    )
    near_o = across(near)
    far_o = across(far)
    inner, inner_o, near_g, near_og, far_g, far_og = probes(
        device, places, live, (own, own_o, near, near_o, far, far_o), measured[0], probe, prop, dft
    )
    far_og = across(far_og)
    near_og = across(near_og)
    far_g = far_g + far_og
    far = swap_far(far_g)
    far_g, near_og, inner_o = lax.optimization_barrier((far_g, near_og, inner_o))
    near = swap_near(near_g + near_og)
    inner = inner + across(inner_o).astype(jnp.float32)
    inner = inner + far.astype(jnp.float32)
    inner, near = lax.optimization_barrier((inner, near))
    return from_lines(add_up(inner, near))[None]


def solution(mesh):
    placed = (
        P("depth", "tile", None, None),
        P(),
        P(),
        P("tile", None, None, None),
        P("tile", None),
        P("tile", None, None, None, None),
    )
    return jax.shard_map(
        local, mesh=mesh, in_specs=placed, out_specs=P("depth", "tile", None, None), check_vma=False
    )
```

```python
import jax
import jax.numpy as jnp
import numpy as np
from jax import lax
from jax.experimental import pallas as pl
from jax.experimental.pallas import tpu as pltpu
from jax.sharding import PartitionSpec as P

SIDE = 256
M = 128
CAP = 5
LW = 2048
LANES = 128
WIDE = SIDE + LANES
BLOCKS = LW // LANES
GROUP = 8
MIB = 1024 * 1024


def dft_planes():
    n = np.arange(SIDE)
    angles = (n[:, None] * n[None, :] % SIDE) * (2.0 * np.pi / SIDE)
    factor = 1.0 / np.sqrt(SIDE)
    return (
        (np.cos(angles) * factor).astype(jnp.bfloat16),
        (-np.sin(angles) * factor).astype(jnp.bfloat16),
    )


def real_form(xp, re, im):
    return xp.concatenate(
        [xp.concatenate([re, -im], axis=1), xp.concatenate([im, re], axis=1)], axis=0
    )


def as_lines(block):
    rows = block.shape[0]
    lines = block.reshape(rows, 2, BLOCKS, LANES).transpose(0, 2, 1, 3)
    return lines.reshape(rows, 2 * BLOCKS, LANES)


def from_lines(lines):
    rows = lines.shape[0]
    block = lines.reshape(rows, BLOCKS, 2, LANES).transpose(0, 2, 1, 3)
    return block.reshape(rows, 2, LW)


LINES = 2 * BLOCKS
PITCH = LINES + GROUP
STEPS = 8
ROWS = M // STEPS


def planes_kernel(lines_ref, planes_ref, held, sems):
    copies = [
        pltpu.make_async_copy(
            lines_ref.at[pl.ds(step * ROWS, ROWS)],
            held.reshape(M, PITCH, LANES).at[pl.ds(step * ROWS, ROWS), pl.ds(0, LINES), :],
            sems.at[step],
        )
        for step in range(STEPS)
    ]
    for copy in copies:
        copy.start()
    for step, copy in enumerate(copies):
        copy.wait()
        rows = slice(step * ROWS, (step + 1) * ROWS)
        for block in range(BLOCKS):
            for part in range(2):
                first = step * ROWS * PITCH + 2 * block + part
                cells = held[pl.ds(first, ROWS, stride=PITCH), :]
                planes_ref[part, rows, block * LANES : (block + 1) * LANES] = cells.astype(
                    jnp.bfloat16
                )


def split_planes(lines):
    return pl.pallas_call(
        planes_kernel,
        out_shape=jax.ShapeDtypeStruct((2, M, LW), jnp.bfloat16),
        in_specs=[pl.BlockSpec(memory_space=pltpu.HBM)],
        out_specs=pl.BlockSpec(memory_space=pltpu.VMEM),
        scratch_shapes=[
            pltpu.VMEM((M * PITCH, LANES), jnp.float32),
            pltpu.SemaphoreType.DMA((STEPS,)),
        ],
        compiler_params=pltpu.CompilerParams(vmem_limit_bytes=8 * MIB),
        name="split_planes",
    )(lines)


def total_kernel(inner_ref, far_ref, lines_ref, held, sems):
    copies = [
        pltpu.make_async_copy(
            held.reshape(M, PITCH, LANES).at[pl.ds(step * ROWS, ROWS), pl.ds(0, LINES), :],
            lines_ref.at[pl.ds(step * ROWS, ROWS)],
            sems.at[step],
        )
        for step in range(STEPS)
    ]
    for step, copy in enumerate(copies):
        rows = slice(step * ROWS, (step + 1) * ROWS)
        for block in range(BLOCKS):
            cols = slice(block * LANES, (block + 1) * LANES)
            for part in range(2):
                cells = inner_ref[part, rows, cols] + far_ref[part, rows, cols].astype(jnp.float32)
                first = step * ROWS * PITCH + 2 * block + part
                held[pl.ds(first, ROWS, stride=PITCH), :] = cells
        copy.start()
    for copy in copies:
        copy.wait()


def add_up(inner, far):
    return pl.pallas_call(
        total_kernel,
        out_shape=jax.ShapeDtypeStruct((M, LINES, LANES), jnp.float32),
        in_specs=[pl.BlockSpec(memory_space=pltpu.VMEM)] * 2,
        out_specs=pl.BlockSpec(memory_space=pltpu.HBM),
        scratch_shapes=[
            pltpu.VMEM((M * PITCH, LANES), jnp.float32),
            pltpu.SemaphoreType.DMA((STEPS,)),
        ],
        compiler_params=pltpu.CompilerParams(vmem_limit_bytes=12 * MIB),
        name="add_up",
    )(inner, far)


def product(a_re, a_im, b_re, b_im):
    return a_re * b_re - a_im * b_im, a_re * b_im + a_im * b_re


def conj_product(a_re, a_im, b_re, b_im):
    return a_re * b_re + a_im * b_im, a_re * b_im - a_im * b_re


def lanes(cells, count):
    return [cells[..., k * LANES : (k + 1) * LANES] for k in range(count)]


def wide(value):
    return value.astype(jnp.float32)


def probes_kernel(
    device_ref,
    places_ref,
    counts_ref,
    own_ref,
    own_o_ref,
    near_ref,
    near_o_ref,
    far_ref,
    far_o_ref,
    observed_ref,
    probe_ref,
    prop_hbm,
    dft_hbm,
    inner_out,
    inner_o_out,
    near_out,
    near_o_out,
    far_out,
    far_o_out,
    cuts,
    observed,
    window,
    object_1,
    psi_1,
    columns,
    rows,
    totals,
    matrices,
    cut_sems,
    observed_sem,
    matrix_sems,
):
    mine = device_ref[0]
    other = 1 - mine
    odd = device_ref[1]
    near_part, far_part = 2 - 2 * odd, 2 * odd

    def place(slot):
        row = places_ref[mine * CAP + slot, 0]
        col = places_ref[mine * CAP + slot, 1]
        base = pl.multiple_of(jnp.minimum(col // LANES, BLOCKS - 3) * LANES, LANES)
        row_base = pl.multiple_of(jnp.minimum(row // GROUP, M // GROUP - 1) * GROUP, GROUP)
        return row, row_base, row - row_base, base, col - base

    places = [place(slot) for slot in range(CAP)]

    def cut_copies(which, slot):
        base = places[slot][3]
        sources = ((near_ref, own_ref, far_ref), (near_o_ref, own_o_ref, far_o_ref))[which]
        return [
            pltpu.make_async_copy(
                source.at[:, :, pl.ds(base, WIDE)],
                cuts.at[(mine, other)[which], slot, part],
                cut_sems.at[which, slot, k],
            )
            for k, (part, source) in enumerate(zip((near_part, 1, far_part), sources))
        ]

    matrix_copies = [
        pltpu.make_async_copy(source, matrices.at[k], matrix_sems.at[k])
        for k, source in enumerate((prop_hbm, dft_hbm))
    ]
    for slot in range(CAP):
        for which in range(2):
            for copy in cut_copies(which, slot):
                copy.start()
        if slot == 0:
            matrix_copies[0].start()
    matrix_copies[1].start()
    prop_ref, prop_t_ref = matrices.at[0, 0], matrices.at[0, 1]
    dft_ref, dft_t_ref = matrices.at[1, 0], matrices.at[1, 1]
    observed_copy = pltpu.make_async_copy(observed_ref.at[mine], observed, observed_sem)
    observed_copy.start()
    totals[...] = jnp.zeros_like(totals)

    rim_row = lax.broadcasted_iota(jnp.int32, (M, WIDE), 0)
    lane_of_rim = lax.broadcasted_iota(jnp.int32, (M, LANES), 1)
    lane = lax.broadcasted_iota(jnp.int32, (SIDE + GROUP, LANES), 1)
    line = lax.broadcasted_iota(jnp.int32, (SIDE // GROUP, GROUP, SIDE), 1)
    line_out = lax.broadcasted_iota(jnp.int32, (1, GROUP, SIDE), 1)

    def cut(slice_no, slot, part):
        row, row_base, row_offset, _, offset = places[slot]
        back = lax.rem(LANES - offset, LANES)
        row_back = lax.rem(GROUP - row_offset, GROUP)
        keep = lane_of_rim < LANES - offset
        held = window.at[slot % 2, part]

        def to_left(cells):
            turned = [pltpu.roll(block, back, 1) for block in lanes(cells, 3)]
            return [jnp.where(keep, turned[k], turned[k + 1]) for k in range(2)]

        rim = to_left(
            wide(
                jnp.where(
                    rim_row >= row,
                    cuts[slice_no, slot, 0, part],
                    cuts[slice_no, slot, 2, part],
                )
            )
        )
        middle = to_left(wide(cuts[slice_no, slot, 1, part]))
        for k in range(2):
            here = slice(k * LANES, (k + 1) * LANES)
            held[0:M, here] = rim[k]
            held[M : 2 * M, here] = middle[k]
            held[2 * M : 3 * M, here] = rim[k]
        cells = held[pl.ds(row_base, SIDE + GROUP), :].reshape(SIDE // GROUP + 1, GROUP, SIDE)
        cells = pltpu.roll(cells, row_back, 1)
        cells = jnp.where(line < GROUP - row_offset, cells[:-1], cells[1:])
        return cells.reshape(SIDE, SIDE)

    def add_patch(slice_no, slot, patch):
        _, row_base, row_offset, base, offset = places[slot]
        row_forth = lax.rem(row_offset, GROUP)
        forth = lax.rem(offset, LANES)
        for part in range(2):
            cells = pltpu.roll(patch[part].reshape(SIDE // GROUP, GROUP, SIDE), row_forth, 1)
            late = line_out >= row_offset
            cells = jnp.concatenate(
                [
                    jnp.where(late, cells[:1], 0.0),
                    jnp.where(line[1:] >= row_offset, cells[1:], cells[:-1]),
                    jnp.where(late, 0.0, cells[-1:]),
                ],
                axis=0,
            ).reshape(SIDE + GROUP, SIDE)
            turned = [pltpu.roll(block, forth, 1) for block in lanes(cells, 2)]
            late = lane >= offset
            spread = jnp.concatenate(
                [
                    jnp.where(late, turned[0], 0.0),
                    jnp.where(late, turned[1], turned[0]),
                    jnp.where(late, 0.0, turned[1]),
                ],
                axis=1,
            )
            totals[slice_no, part, pl.ds(row_base, SIDE + GROUP), pl.ds(base, WIDE)] += spread

    def to_columns(slot, wave, matrix):
        for part in range(2):
            columns[part * SIDE : (part + 1) * SIDE, slot * SIDE : (slot + 1) * SIDE] = wave[part].astype(jnp.bfloat16)
        if slot < CAP - 1:
            return
        middle = jnp.dot(matrix[...], columns[...], preferred_element_type=jnp.float32)
        for k in range(CAP):
            for part in range(2):
                rows[k, :, part * SIDE : (part + 1) * SIDE] = middle[
                    part * SIDE : (part + 1) * SIDE, k * SIDE : (k + 1) * SIDE
                ].astype(jnp.bfloat16)

    def from_rows(slot, matrix):
        result = jnp.dot(rows[slot], matrix[...], preferred_element_type=jnp.float32)
        return result[:, :SIDE], result[:, SIDE:]

    def rounded(wave):
        return tuple(wide(plane.astype(jnp.bfloat16)) for plane in wave)

    def psi_0():
        return wide(probe_ref[0]), wide(probe_ref[1])

    def held_pair(ref, slot):
        return wide(ref[slot, 0]), wide(ref[slot, 1])

    for slot in range(CAP):
        for which in range(2):
            for copy in cut_copies(which, slot):
                copy.wait()
        phi = product(*psi_0(), cut(0, slot, 0), cut(0, slot, 1))
        if slot == 0:
            matrix_copies[0].wait()
        to_columns(slot, phi, prop_ref)
    matrix_copies[1].wait()
    for slot in range(CAP):
        for part in range(2):
            object_1[slot, part] = cut(1, slot, part).astype(jnp.bfloat16)
        wave = from_rows(slot, prop_t_ref)
        for part in range(2):
            psi_1[slot, part] = wave[part].astype(jnp.bfloat16)
        phi = product(*rounded(wave), *held_pair(object_1, slot))
        to_columns(slot, phi, dft_ref)
    observed_copy.wait()
    for slot in range(CAP):
        far_re, far_im = from_rows(slot, dft_t_ref)
        live = (slot < counts_ref[mine]).astype(jnp.float32)
        misfit = live * (far_re * far_re + far_im * far_im - observed[slot])
        to_columns(slot, (misfit * far_re, misfit * far_im), dft_t_ref)
    for slot in range(CAP):
        spread = rounded(from_rows(slot, dft_ref))
        to_columns(slot, conj_product(*held_pair(object_1, slot), *spread), prop_t_ref)
        add_patch(1, slot, conj_product(*held_pair(psi_1, slot), *spread))
    for slot in range(CAP):
        spread = rounded(from_rows(slot, prop_ref))
        add_patch(0, slot, conj_product(*psi_0(), *spread))

    def narrow(slice_no, first_row):
        return totals[slice_no, :, pl.ds(first_row, M), :].astype(jnp.bfloat16)

    near_row = pl.multiple_of(near_part * M, M)
    far_row = pl.multiple_of(far_part * M, M)
    far_o_out[...] = narrow(other, far_row)
    near_o_out[...] = narrow(other, near_row)
    far_out[...] = narrow(mine, far_row)
    near_out[...] = narrow(mine, near_row)
    inner_o_out[...] = narrow(other, M)
    inner_out[...] = totals[mine, :, M : 2 * M, :]


def probes(device, places, counts, planes, observed, probe, prop, dft):
    smem = pl.BlockSpec(memory_space=pltpu.SMEM)
    vmem = pl.BlockSpec(memory_space=pltpu.VMEM)
    apart = pl.BlockSpec(memory_space=pl.ANY)
    rim = jax.ShapeDtypeStruct((2, M, LW), jnp.bfloat16)
    return pl.pallas_call(
        probes_kernel,
        out_shape=[jax.ShapeDtypeStruct((2, M, LW), jnp.float32)] + [rim] * 5,
        in_specs=[smem] * 3 + [apart] * 7 + [vmem, apart, apart],
        out_specs=[vmem] * 6,
        scratch_shapes=[
            pltpu.VMEM((2, CAP, 3, 2, M, WIDE), jnp.bfloat16),
            pltpu.VMEM((CAP, SIDE, SIDE), jnp.float32),
            pltpu.VMEM((2, 2, 3 * M, SIDE), jnp.float32),
            pltpu.VMEM((CAP, 2, SIDE, SIDE), jnp.bfloat16),
            pltpu.VMEM((CAP, 2, SIDE, SIDE), jnp.bfloat16),
            pltpu.VMEM((2 * SIDE, CAP * SIDE), jnp.bfloat16),
            pltpu.VMEM((CAP, SIDE, 2 * SIDE), jnp.bfloat16),
            pltpu.VMEM((2, 2, 3 * M, LW), jnp.float32),
            pltpu.VMEM((2, 2, 2 * SIDE, 2 * SIDE), jnp.bfloat16),
            pltpu.SemaphoreType.DMA((2, CAP, 3)),
            pltpu.SemaphoreType.DMA,
            pltpu.SemaphoreType.DMA((2,)),
        ],
        compiler_params=pltpu.CompilerParams(vmem_limit_bytes=38 * MIB),
        name="probes",
    )(device, places, counts, *planes, observed, probe, prop, dft)


def swap_near(value):
    count = lax.axis_size("tile")
    return lax.ppermute(value, "tile", [(t, t ^ 1) for t in range(count)])


def swap_far(value):
    count = lax.axis_size("tile")
    pairs = [(t, t + 1) for t in range(1, count - 1, 2)]
    return lax.ppermute(value, "tile", pairs + [(b, a) for a, b in pairs])


def across(value):
    return lax.ppermute(value, "depth", [(0, 1), (1, 0)])


def local(object_layer_slices, probe_wave, propagator, positions, counts, measured):
    lines = pltpu.with_memory_space_constraint(as_lines(object_layer_slices[0]), pltpu.HBM)
    own = split_planes(lines)
    near = swap_near(own)
    far = swap_far(own)
    own_o = across(own)

    device = jnp.stack([lax.axis_index("depth"), lax.axis_index("tile") % 2]).astype(jnp.int32)
    probe = jnp.stack([probe_wave[:, 0], probe_wave[:, 1]])
    prop = real_form(jnp, propagator[:, 0], propagator[:, 1])
    prop = jnp.stack([prop, prop.T])
    dft = real_form(np, *dft_planes())
    dft = jnp.asarray(np.stack([dft, dft.T]))
    near, probe, prop, places, live, device = lax.optimization_barrier(
        (near, probe, prop, positions.reshape(2 * CAP, 2), counts.reshape(2), device)
    )
    near_o = across(near)
    far_o = across(far)
    inner, inner_o, near_g, near_og, far_g, far_og = probes(
        device, places, live, (own, own_o, near, near_o, far, far_o), measured[0], probe, prop, dft
    )
    far_og = across(far_og)
    near_og = across(near_og)
    far_g = far_g + far_og
    far = swap_far(far_g)
    far_g, near_og, inner_o = lax.optimization_barrier((far_g, near_og, inner_o))
    near = swap_near(near_g + near_og)
    inner = inner + across(inner_o).astype(jnp.float32)
    inner = inner + far.astype(jnp.float32)
    inner, near = lax.optimization_barrier((inner, near))
    return from_lines(add_up(inner, near))[None]


def solution(mesh):
    placed = (
        P("depth", "tile", None, None),
        P(),
        P(),
        P("tile", None, None, None),
        P("tile", None),
        P("tile", None, None, None, None),
    )
    return jax.shard_map(
        local, mesh=mesh, in_specs=placed, out_specs=P("depth", "tile", None, None), check_vma=False
    )
```
